32 devices in a mesh: row: 16 (over z, y, x), col: 2 (over core).
Axes of the slice: x: 2, y: 2, z: 4, core: 2. Of those that a mesh axis runs over, the one named last changes fastest.
Arguments:
- descriptors: bfloat16 [4096, 20480], P('row', 'col')
- block_mask: int32 [32, 160], P('row', 'col'), may hold values 0 or 1
- config_of: int32 [4096], P('row'), may hold values from 0 to 1023, as said below
Outputs:
- gram: float32 [384, 20480], P('row', 'col')
The draws below stay inside these ranges and needn't reach their ends.
Inputs may be any that keep to these rules, and one draw needn't show every extreme that they name: `config_of`: each source device's 256 environments name every owner index of row equally often, 256 // 16 times.
All inputs are finite; a program needn't handle non-finite values. No bound on the sum of `block_mask` on one device may be relied on, other than what follows from the above.
Results may differ from the reference program's by a relative error of at most 0.0024.
Values may be sent and summed in bfloat16 or wider, within the bound.
A program may use at most 64 MiB of HBM per device.

```python
import math
import jax
import jax.numpy as jnp
from jax import lax

COLS = 20480
BLOCK = 128
PW = 384
ROW_DEV = 256
CONF_DEV = 64
ROWS = 4096
N_ROW = 16
N_COL = 2


def draw_config_of(key, part):
    devices = ROWS // ROW_DEV
    base = jnp.repeat(jnp.arange(devices, dtype=jnp.int32), ROW_DEV // devices)
    keys = jax.random.split(jax.random.fold_in(key, 1), devices)
    slabs = jax.vmap(lambda k: jax.random.permutation(k, base))(keys).reshape(ROWS)
    local = jax.random.randint(jax.random.fold_in(key, 2), (ROWS,), 0, CONF_DEV, dtype=jnp.int32)
    return slabs * CONF_DEV + local


def draw_descriptors(key, part):
    k_vals = jax.random.fold_in(key, 11)
    k_cols = jax.random.fold_in(key, 12)
    column = jnp.exp(jax.random.uniform(k_cols, (COLS,), jnp.float32, math.log(0.3), math.log(3.0)))
    values = jax.random.normal(k_vals, (ROWS, COLS), jnp.float32)
    return (values * column[None, :]).astype(jnp.bfloat16)


def set_ends(result, key, least, high):
    longest = result.shape.index(max(result.shape))
    spots = []
    for shift in (0, 1):
        where = [jax.random.randint(jax.random.fold_in(key, axis), (), 0, length) for axis, length in enumerate(result.shape)]
        where[longest] = (where[longest] + shift) % result.shape[longest]
        spots.append(tuple(where))
    return result.at[spots[0]].set(least).at[spots[1]].set(high)


def setup_inputs(seed: int = 0) -> dict:
    arg_keys = jax.random.split(jax.random.key(seed), 4)
    descriptors = draw_descriptors(jax.random.fold_in(arg_keys[3], 71), 0)
    block_mask = set_ends((jax.random.randint(arg_keys[1], (ROWS // BLOCK, COLS // BLOCK), 0, 4) < 3).astype(jnp.int32), jax.random.fold_in(arg_keys[1], 1), 0, 1)
    config_of = draw_config_of(jax.random.fold_in(arg_keys[3], 71), 0)
    return dict(descriptors=descriptors, block_mask=block_mask, config_of=config_of)


def reference(descriptors, block_mask, config_of):
    width = COLS // N_COL
    part = PW // N_COL
    configs = CONF_DEV * N_ROW
    counts = jax.ops.segment_sum(jnp.ones((ROWS,), jnp.float32), config_of, configs)
    row_mask = jnp.repeat(block_mask, BLOCK, axis=0).astype(jnp.bfloat16)

    def center(group):
        span = lax.dynamic_slice_in_dim(descriptors, group * width, width, 1)
        marks = lax.dynamic_slice_in_dim(row_mask, group * (width // BLOCK), width // BLOCK, 1)
        masked = (span.reshape(ROWS, width // BLOCK, BLOCK) * marks[:, :, None]).reshape(ROWS, width)
        sums = jax.ops.segment_sum(masked.astype(jnp.float32), config_of, configs)
        means = sums / jnp.maximum(counts, 1.0)[:, None]
        return (masked.astype(jnp.float32) - means[config_of]).astype(jnp.bfloat16)

    groups = jnp.arange(N_COL, dtype=jnp.int32)
    pieces = lax.map(lambda g: center(g)[:, :part], groups)
    panel = jnp.moveaxis(pieces, 0, 1).reshape(ROWS, PW)

    def gram_group(group):
        return jnp.dot(panel.T, center(group), preferred_element_type=jnp.float32) * (1.0 / ROWS)

    grams = lax.map(gram_group, groups)
    return jnp.moveaxis(grams, 0, 1).reshape(PW, COLS)
```

```python
import functools
import math

import jax
import jax.numpy as jnp
from jax import lax
from jax.experimental import pallas as pl
from jax.experimental.pallas import tpu as pltpu
from jax.sharding import PartitionSpec as P

PW = 384
CONF_DEV = 64
BLOCK = 128
G = 4
SLOT = 16
F32 = jnp.float32
BF16 = jnp.bfloat16


def remote(src, dst, send, recv, **where):
    return pltpu.make_async_remote_copy(
        src_ref=src, dst_ref=dst, send_sem=send, recv_sem=recv,
        device_id=where, device_id_type=pl.DeviceIdType.MESH,
    )


def kernel(cfg, pext, ocol, orow, marks, x, out,
           perm, asend, arec, bsend, brec, piece, hl, mrec, xrec, xmask, part_sum, from_low, from_high, fin,
           a_s, a_r, b_s, b_r, p_s, p_r, c_s, c_r, m_s, m_r, x_s, x_r, lo_s, lo_r, hi_s, hi_r, f_s, f_r, l_s):
    n, ncol, rows, width, part, wide, tiles, tw, factor = cfg
    line = n // G
    per_plane = PW // line
    per_dev = PW // n
    chunk = width // G
    r = lax.axis_index("row")
    c = lax.axis_index("col")
    z = r // G
    q = r % G

    barrier = pltpu.get_barrier_semaphore()

    @pl.loop(1, n)
    def _(k):
        pl.semaphore_signal(barrier, inc=1, device_id={"row": (r + k) % n}, device_id_type=pl.DeviceIdType.MESH)

    @pl.loop(1, ncol)
    def _(k):
        pl.semaphore_signal(barrier, inc=1, device_id={"col": (c + k) % ncol}, device_id_type=pl.DeviceIdType.MESH)

    first = lax.broadcasted_iota(jnp.int32, (rows, rows), 0)
    second = lax.broadcasted_iota(jnp.int32, (rows, rows), 1)
    before = (ocol[...] == orow[...]) & (first < second)
    rank = jnp.sum(jnp.where(before, 1.0, 0.0), axis=0, keepdims=True)
    place = orow[...].astype(F32) * SLOT + rank
    slots = lax.broadcasted_iota(jnp.int32, (n * SLOT, rows), 0).astype(F32)
    perm[...] = jnp.where(slots == place, 1.0, 0.0).astype(BF16)
    asend[...] = jnp.dot(perm[...], pext[...], preferred_element_type=F32).astype(BF16)
    pl.semaphore_wait(barrier, n - 1 + ncol - 1)

    def slot_rows(k):
        return pl.ds(pl.multiple_of(k * SLOT, SLOT), SLOT)

    def to_owner(k):
        peer = (r + k) % n
        return remote(asend.at[slot_rows(peer), :], arec.at[slot_rows(r), :], a_s.at[k], a_r.at[r], row=peer)

    def from_source(k):
        peer = (r + k) % n
        return remote(asend.at[slot_rows(peer), :], arec.at[slot_rows(peer), :], a_s.at[k], a_r.at[peer], row=peer)

    def to_source(k):
        peer = (r + k) % n
        return remote(bsend.at[slot_rows(peer), :], brec.at[slot_rows(r), :], b_s.at[k], b_r.at[r], row=peer)

    def from_owner(k):
        peer = (r + k) % n
        return remote(bsend.at[slot_rows(peer), :], brec.at[slot_rows(peer), :], b_s.at[k], b_r.at[peer], row=peer)

    def x_cols(dest, t):
        return pl.ds(pl.multiple_of(dest * chunk + t * tw, BLOCK), tw)

    def src_rows(s):
        return pl.ds(pl.multiple_of(s * rows, BLOCK), rows)

    def x_send(t, k):
        mate = (q + k) % G
        return remote(x.at[:, x_cols(mate, t)], xrec.at[t, src_rows(q), :], x_s.at[t, k], x_r.at[t, q], row=z * G + mate)

    def x_from(t, k):
        mate = (q + k) % G
        return remote(x.at[:, x_cols(mate, t)], xrec.at[t, src_rows(mate), :], x_s.at[t, k], x_r.at[t, mate], row=z * G + mate)

    def x_own(t):
        return pltpu.make_async_copy(x.at[:, x_cols(q, t)], xrec.at[t, src_rows(q), :], x_s.at[t, 0])

    def m_send(k):
        mate = (q + k) % G
        return remote(marks.at[mate], mrec.at[q], m_s.at[k], m_r.at[q], row=z * G + mate)

    def m_from(k):
        mate = (q + k) % G
        return remote(marks.at[mate], mrec.at[mate], m_s.at[k], m_r.at[mate], row=z * G + mate)

    def hl_slot(col, s):
        return hl.at[:, pl.ds(pl.multiple_of(col * part, 16), part), src_rows(s)]

    def p_send(k):
        mate = (q + k) % G
        return remote(piece, hl_slot(c, q), p_s.at[k], p_r.at[q], row=z * G + mate)

    def p_from(k):
        mate = (q + k) % G
        return remote(piece, hl_slot(c, mate), p_s.at[k], p_r.at[mate], row=z * G + mate)

    def c_own(j):
        peer = (c + j) % ncol
        return remote(piece, hl_slot(c, q), c_s.at[j, 0], c_r.at[c, q], col=peer)

    def c_relay(j, k):
        peer = (c + j) % ncol
        mate = (q + k) % G
        return remote(hl_slot(c, mate), hl_slot(c, mate), c_s.at[j, k], c_r.at[c, mate], col=peer)

    def c_from(j, k):
        peer = (c + j) % ncol
        mate = (q + k) % G
        return remote(piece, hl_slot(peer, mate), c_s.at[j, k], c_r.at[peer, mate], col=peer)

    own_a = pltpu.make_async_copy(asend.at[slot_rows(r), :], arec.at[slot_rows(r), :], l_s.at[0])
    own_a.start()

    @pl.loop(1, n)
    def _(k):
        to_owner(k).start()

    own_m = pltpu.make_async_copy(marks.at[q], mrec.at[q], l_s.at[1])
    own_m.start()
    for k in range(1, G):
        m_send(k).start()

    def start_x(t):
        for k in (2, 1, 3):
            x_send(t, k).start()
        x_own(t).start()

    start_x(0)

    own_a.wait()

    @pl.loop(1, n)
    def _(k):
        from_source(k).wait_recv()

    arrived = arec[...]
    label = arrived[:, part:part + 1].astype(F32)
    ids = lax.broadcasted_iota(jnp.int32, (n * SLOT, BLOCK), 1).astype(F32) + 1.0
    member = jnp.where((label == ids) & (ids <= CONF_DEV), 1.0, 0.0).astype(BF16)
    same = lax.dot_general(member, member, (((1,), (1,)), ((), ())), preferred_element_type=F32)
    counts = jnp.maximum(jnp.sum(same, axis=1, keepdims=True), 1.0)
    same = same.astype(BF16)
    means = jnp.dot(same, arrived, preferred_element_type=F32) / counts
    high = (arrived.astype(F32) - means).astype(BF16)
    low = -(jnp.dot(same, high, preferred_element_type=F32) / counts)
    bsend[:, :wide] = high
    bsend[:, wide:] = low.astype(BF16)

    own_b = pltpu.make_async_copy(bsend.at[slot_rows(r), :], brec.at[slot_rows(r), :], l_s.at[2])
    own_b.start()

    @pl.loop(1, n)
    def _(k):
        to_source(k).start()

    start_x(1)
    own_b.wait()

    @pl.loop(1, n)
    def _(k):
        from_owner(k).wait_recv()

    back = lax.dot_general(brec[...], perm[...], (((0,), (0,)), ((), ())), preferred_element_type=F32).astype(BF16)
    piece[0] = back[:part]
    piece[1] = back[wide:wide + part]
    own_p = pltpu.make_async_copy(piece, hl_slot(c, q), l_s.at[3])
    own_p.start()
    for k in (2, 1, 3):
        p_send(k).start()

    @pl.loop(1, ncol)
    def _(j):
        c_own(j).start()

    for t in range(2, tiles):
        start_x(t)

    for k in (1, 3, 2):
        p_from(k).wait_recv()

        @pl.loop(1, ncol)
        def _(j, k=k):
            c_relay(j, k).start()

    own_p.wait()
    own_m.wait()
    for k in range(1, G):
        m_from(k).wait_recv()

    @pl.loop(1, ncol)
    def _(j):
        for k in range(G):
            c_from(j, k).wait_recv()

    def rows_of(a):
        return pl.ds(pl.multiple_of(a * per_plane, 8), per_plane)

    def up(t, a):
        return remote(part_sum.at[t, rows_of(a), :], from_low.at[t, rows_of(a), :],
                      lo_s.at[t, a], lo_r.at[t, a], row=(r + G) % n)

    def down(t, a):
        return remote(part_sum.at[t, rows_of(a), :], from_high.at[t, rows_of(a), :],
                      hi_s.at[t, a], hi_r.at[t, a], row=(r + n - G) % n)

    def f_send(t, k):
        mate = (q + k) % G
        return remote(fin.at[t, mate], out.at[:, x_cols(q, t)], f_s.at[t, k], f_r.at[t, q], row=z * G + mate)

    def f_from(t, k):
        mate = (q + k) % G
        return remote(fin.at[t, mate], out.at[:, x_cols(mate, t)], f_s.at[t, k], f_r.at[t, mate], row=z * G + mate)

    def f_own(t):
        return pltpu.make_async_copy(fin.at[t, q], out.at[:, x_cols(q, t)], f_s.at[t, 0])

    def multiply(t):
        x_own(t).wait()
        for k in (1, 3, 2):
            x_from(t, k).wait_recv()
        for s in range(G):
            for b in range(rows // BLOCK):
                span = slice(s * rows + b * BLOCK, s * rows + (b + 1) * BLOCK)
                for w in range(tw // BLOCK):
                    cols = slice(w * BLOCK, (w + 1) * BLOCK)
                    keep = jnp.broadcast_to(mrec[s, t, b:b + 1, w:w + 1], (BLOCK, BLOCK)).astype(BF16)
                    xmask[span, cols] = xrec[t, span, cols] * keep
        part_sum[t] = jnp.dot(hl[0], xmask[...], preferred_element_type=F32) + jnp.dot(
            hl[1], xmask[...], preferred_element_type=F32)

    def forward(t):
        def go_up(i, carry):
            a = line - 1 - i

            @pl.when(z > 0)
            def _():
                up(t, a).wait_recv()
                part_sum[t, rows_of(a), :] += from_low[t, rows_of(a), :]

            up(t, a).start()
            return carry

        lax.fori_loop(0, line - 1 - z, go_up, 0)

        def go_down(a, carry):
            @pl.when(z < line - 1)
            def _():
                down(t, a).wait_recv()
                part_sum[t, rows_of(a), :] += from_high[t, rows_of(a), :]

            down(t, a).start()
            return carry

        lax.fori_loop(0, z, go_down, 0)

    def finish(t):
        @pl.when(z > 0)
        def _():
            up(t, z).wait_recv()
            part_sum[t, rows_of(z), :] += from_low[t, rows_of(z), :]

        @pl.when(z < line - 1)
        def _():
            down(t, z).wait_recv()
            part_sum[t, rows_of(z), :] += from_high[t, rows_of(z), :]

        total = part_sum[t, rows_of(z), :] * factor
        for s in range(G):
            fin[t, s] = total[s * per_dev:(s + 1) * per_dev]
        f_own(t).start()
        for k in (2, 1, 3):
            f_send(t, k).start()

    def step(t, carry):
        multiply(t)
        forward(t)

        @pl.when(t > 0)
        def _():
            finish(t - 1)

        return carry

    lax.fori_loop(0, tiles, step, 0)
    finish(tiles - 1)

    @pl.loop(0, tiles)
    def _(t):
        f_own(t).wait()
        for k in range(1, G):
            f_from(t, k).wait_recv()
            f_send(t, k).wait_send()
            x_send(t, k).wait_send()

        def sent_up(a, carry):
            up(t, a).wait_send()
            return carry

        def sent_down(a, carry):
            down(t, a).wait_send()
            return carry

        lax.fori_loop(z + 1, line, sent_up, 0)
        lax.fori_loop(0, z, sent_down, 0)

    for k in range(1, G):
        m_send(k).wait_send()
        p_send(k).wait_send()

    @pl.loop(1, ncol)
    def _(j):
        c_own(j).wait_send()
        for k in range(1, G):
            c_relay(j, k).wait_send()

    @pl.loop(1, n)
    def _(k):
        to_owner(k).wait_send()
        to_source(k).wait_send()


def body(descriptors, block_mask, config_of):
    n, ncol = lax.axis_size("row"), lax.axis_size("col")
    rows, width = descriptors.shape
    row_blocks, blocks = block_mask.shape
    part = PW // ncol
    wide = -(-(part + 1) // 128) * 128
    chunk_blocks = blocks // G
    tiles = 5 if chunk_blocks % 5 == 0 else 1
    per_tile = chunk_blocks // tiles
    tw = per_tile * BLOCK
    line = n // G
    per_dev = PW // n

    panel = descriptors[:, :part]
    panel_marks = jnp.repeat(jnp.repeat(block_mask.astype(BF16), BLOCK, axis=0), BLOCK, axis=1)[:, :part]
    label = (config_of % CONF_DEV + 1).astype(BF16)[:, None]
    pext = jnp.concatenate([panel * panel_marks, label, jnp.zeros((rows, wide - part - 1), BF16)], axis=1)
    owner = config_of // CONF_DEV
    marks = block_mask.astype(F32).reshape(row_blocks, G, tiles, per_tile).transpose(1, 2, 0, 3)
    marks = jnp.pad(marks, ((0, 0), (0, 0), (0, 8 - row_blocks), (0, 128 - per_tile)))

    cfg = (n, ncol, rows, width, part, wide, tiles, tw, 1.0 / (rows * n))
    vm = pltpu.VMEM
    dma = pltpu.SemaphoreType.DMA
    full = pl.BlockSpec(memory_space=pltpu.VMEM)
    return pl.pallas_call(
        functools.partial(kernel, cfg),
        out_shape=jax.ShapeDtypeStruct((per_dev, width), F32),
        in_specs=[full, full, full, full, pl.BlockSpec(memory_space=pl.ANY)],
        out_specs=full,
        scratch_shapes=[
            vm((n * SLOT, rows), BF16),
            vm((n * SLOT, wide), BF16),
            vm((n * SLOT, wide), BF16),
            vm((n * SLOT, 2 * wide), BF16),
            vm((n * SLOT, 2 * wide), BF16),
            vm((2, part, rows), BF16),
            vm((2, PW, G * rows), BF16),
            vm((G, tiles, 8, 128), F32),
            vm((tiles, G * rows, tw), BF16),
            vm((G * rows, tw), BF16),
            vm((tiles, PW, tw), F32),
            vm((tiles, PW, tw), F32),
            vm((tiles, PW, tw), F32),
            vm((tiles, G, per_dev, tw), F32),
            dma((n,)), dma((n,)), dma((n,)), dma((n,)),
            dma((G,)), dma((G,)), dma((ncol, G)), dma((ncol, G)),
            dma((G,)), dma((G,)), dma((tiles, G)), dma((tiles, G)),
            dma((tiles, line)), dma((tiles, line)), dma((tiles, line)), dma((tiles, line)),
            dma((tiles, G)), dma((tiles, G)), dma((4,)),
        ],
        compiler_params=pltpu.CompilerParams(
            collective_id=0, has_side_effects=True, vmem_limit_bytes=56 * 1024 * 1024),
    )(pext, owner[:, None], owner[None, :], marks, descriptors)


def solution(mesh):
    in_specs = (P("row", "col"), P("row", "col"), P("row"))
    out_specs = P("row", "col")
    return jax.shard_map(body, mesh=mesh, in_specs=in_specs, out_specs=out_specs, check_vma=False)
```

```python
import functools
import math

import jax
import jax.numpy as jnp
from jax import lax
from jax.experimental import pallas as pl
from jax.experimental.pallas import tpu as pltpu
from jax.sharding import PartitionSpec as P

PW = 384
CONF_DEV = 64
BLOCK = 128
G = 4
SLOT = 16
TILES = 10
AHEAD = (0, 1)
HALF = True
F32 = jnp.float32
BF16 = jnp.bfloat16


def remote(src, dst, send, recv, **where):
    return pltpu.make_async_remote_copy(
        src_ref=src, dst_ref=dst, send_sem=send, recv_sem=recv,
        device_id=where, device_id_type=pl.DeviceIdType.MESH,
    )


def kernel(cfg, ccol, crow, marks, x, out,
           pext, perm, asend, arec, bsend, brec, piece, hl, mrec, xrec, xmask, part_sum, from_low, from_high, fin,
           a_s, a_r, b_s, b_r, p_s, p_r, c_s, c_r, m_s, m_r, x_s, x_r, lo_s, lo_r, hi_s, hi_r, f_s, f_r, l_s, half_sum, half_low, half_high):
    n, ncol, rows, width, part, wide, tiles, tw, factor = cfg
    line = n // G
    per_plane = PW // line
    per_dev = PW // n
    chunk = width // G
    chunk_blocks = chunk // BLOCK
    r = lax.axis_index("row")
    c = lax.axis_index("col")
    z = r // G
    q = r % G

    panel_copy = pltpu.make_async_copy(x.at[:, :wide], pext, l_s.at[4])
    panel_copy.start()
    barrier = pltpu.get_barrier_semaphore()

    @pl.loop(1, n)
    def _(k):
        pl.semaphore_signal(barrier, inc=1, device_id={"row": (r + k) % n}, device_id_type=pl.DeviceIdType.MESH)

    @pl.loop(1, ncol)
    def _(k):
        pl.semaphore_signal(barrier, inc=1, device_id={"col": (c + k) % ncol}, device_id_type=pl.DeviceIdType.MESH)

    first = lax.broadcasted_iota(jnp.int32, (rows, rows), 0)
    second = lax.broadcasted_iota(jnp.int32, (rows, rows), 1)
    shift = CONF_DEV.bit_length() - 1
    owner = crow[...] >> shift
    before = ((ccol[...] >> shift) == owner) & (first < second)
    rank = jnp.sum(jnp.where(before, 1.0, 0.0), axis=0, keepdims=True)
    place = owner.astype(F32) * SLOT + rank
    slots = lax.broadcasted_iota(jnp.int32, (n * SLOT, rows), 0).astype(F32)
    perm[...] = jnp.where(slots == place, 1.0, 0.0).astype(BF16)
    panel_copy.wait()
    label = ((ccol[...] & (CONF_DEV - 1)) + 1).astype(F32)
    lane = lax.broadcasted_iota(jnp.int32, (BLOCK, BLOCK), 1)
    per_tile = tw // BLOCK
    for b in range(rows // BLOCK):
        span = slice(b * BLOCK, (b + 1) * BLOCK)
        for w in range(wide // BLOCK):
            cols = slice(w * BLOCK, (w + 1) * BLOCK)
            keep = jnp.zeros((1, 1), F32)
            if w * BLOCK < part:
                keep = marks[w // chunk_blocks, w % chunk_blocks // per_tile, b:b + 1, w % per_tile:w % per_tile + 1]
            block = pext[span, cols].astype(F32) * jnp.broadcast_to(keep, (BLOCK, BLOCK))
            if (w + 1) * BLOCK > part:
                block = jnp.where(lane + w * BLOCK < part, block, jnp.broadcast_to(label[span], (BLOCK, BLOCK)))
            pext[span, cols] = block.astype(BF16)
    asend[...] = jnp.dot(perm[...], pext[...], preferred_element_type=F32).astype(BF16)
    pl.semaphore_wait(barrier, n - 1 + ncol - 1)

    def slot_rows(k):
        return pl.ds(pl.multiple_of(k * SLOT, SLOT), SLOT)

    def to_owner(k):
        peer = (r + k) % n
        return remote(asend.at[slot_rows(peer), :], arec.at[slot_rows(r), :], a_s.at[k], a_r.at[r], row=peer)

    def from_source(k):
        peer = (r + k) % n
        return remote(asend.at[slot_rows(peer), :], arec.at[slot_rows(peer), :], a_s.at[k], a_r.at[peer], row=peer)

    def to_source(k):
        peer = (r + k) % n
        return remote(bsend.at[slot_rows(peer), :], brec.at[slot_rows(r), :], b_s.at[k], b_r.at[r], row=peer)

    def from_owner(k):
        peer = (r + k) % n
        return remote(bsend.at[slot_rows(peer), :], brec.at[slot_rows(peer), :], b_s.at[k], b_r.at[peer], row=peer)

    def x_cols(dest, t):
        return pl.ds(pl.multiple_of(dest * chunk + t * tw, BLOCK), tw)

    def src_rows(s):
        return pl.ds(pl.multiple_of(s * rows, BLOCK), rows)

    def x_send(t, k):
        mate = (q + k) % G
        return remote(x.at[:, x_cols(mate, t)], xrec.at[t, src_rows(q), :], x_s.at[t, k], x_r.at[t, q], row=z * G + mate)

    def x_from(t, k):
        mate = (q + k) % G
        return remote(x.at[:, x_cols(mate, t)], xrec.at[t, src_rows(mate), :], x_s.at[t, k], x_r.at[t, mate], row=z * G + mate)

    def x_own(t):
        return pltpu.make_async_copy(x.at[:, x_cols(q, t)], xrec.at[t, src_rows(q), :], x_s.at[t, 0])

    def m_send(k):
        mate = (q + k) % G
        return remote(marks.at[mate], mrec.at[q], m_s.at[k], m_r.at[q], row=z * G + mate)

    def m_from(k):
        mate = (q + k) % G
        return remote(marks.at[mate], mrec.at[mate], m_s.at[k], m_r.at[mate], row=z * G + mate)

    def hl_slot(col, s):
        return hl.at[:, pl.ds(pl.multiple_of(col * part, 16), part), src_rows(s)]

    def p_send(k):
        mate = (q + k) % G
        return remote(piece, hl_slot(c, q), p_s.at[k], p_r.at[q], row=z * G + mate)

    def p_from(k):
        mate = (q + k) % G
        return remote(piece, hl_slot(c, mate), p_s.at[k], p_r.at[mate], row=z * G + mate)

    def c_own(j):
        peer = (c + j) % ncol
        return remote(piece, hl_slot(c, q), c_s.at[j, 0], c_r.at[c, q], col=peer)

    def c_relay(j, k):
        peer = (c + j) % ncol
        mate = (q + k) % G
        return remote(hl_slot(c, mate), hl_slot(c, mate), c_s.at[j, k], c_r.at[c, mate], col=peer)

    def c_from(j, k):
        peer = (c + j) % ncol
        mate = (q + k) % G
        return remote(piece, hl_slot(peer, mate), c_s.at[j, k], c_r.at[peer, mate], col=peer)

    own_a = pltpu.make_async_copy(asend.at[slot_rows(r), :], arec.at[slot_rows(r), :], l_s.at[0])
    own_a.start()

    @pl.loop(1, n)
    def _(k):
        to_owner(k).start()

    own_m = pltpu.make_async_copy(marks.at[q], mrec.at[q], l_s.at[1])
    own_m.start()
    for k in range(1, G):
        m_send(k).start()

    def start_x(t):
        for k in (2, 1, 3):
            x_send(t, k).start()
        x_own(t).start()

    for t in range(AHEAD[0]):
        start_x(t)

    own_a.wait()

    @pl.loop(1, n)
    def _(k):
        from_source(k).wait_recv()

    arrived = arec[...]
    label = arrived[:, part:part + 1].astype(F32)
    ids = lax.broadcasted_iota(jnp.int32, (n * SLOT, BLOCK), 1).astype(F32) + 1.0
    member = jnp.where((label == ids) & (ids <= CONF_DEV), 1.0, 0.0).astype(BF16)
    same = lax.dot_general(member, member, (((1,), (1,)), ((), ())), preferred_element_type=F32)
    counts = jnp.maximum(jnp.sum(same, axis=1, keepdims=True), 1.0)
    same = same.astype(BF16)
    means = jnp.dot(same, arrived, preferred_element_type=F32) / counts
    high = (arrived.astype(F32) - means).astype(BF16)
    low = -(jnp.dot(same, high, preferred_element_type=F32) / counts)
    bsend[:, :wide] = high
    bsend[:, wide:] = low.astype(BF16)

    own_b = pltpu.make_async_copy(bsend.at[slot_rows(r), :], brec.at[slot_rows(r), :], l_s.at[2])
    own_b.start()

    @pl.loop(1, n)
    def _(k):
        to_source(k).start()

    for t in range(AHEAD[0], AHEAD[1]):
        start_x(t)
    own_b.wait()

    @pl.loop(1, n)
    def _(k):
        from_owner(k).wait_recv()

    back = lax.dot_general(brec[...], perm[...], (((0,), (0,)), ((), ())), preferred_element_type=F32).astype(BF16)
    piece[0] = back[:part]
    piece[1] = back[wide:wide + part]
    own_p = pltpu.make_async_copy(piece, hl_slot(c, q), l_s.at[3])
    own_p.start()
    for k in (2, 1, 3):
        p_send(k).start()

    @pl.loop(1, ncol)
    def _(j):
        c_own(j).start()

    for t in range(AHEAD[1], tiles):
        start_x(t)

    for k in (1, 3, 2):
        p_from(k).wait_recv()

        @pl.loop(1, ncol)
        def _(j, k=k):
            c_relay(j, k).start()

    own_p.wait()
    own_m.wait()
    for k in range(1, G):
        m_from(k).wait_recv()

    @pl.loop(1, ncol)
    def _(j):
        for k in range(G):
            c_from(j, k).wait_recv()

    def rows_of(a):
        return pl.ds(pl.multiple_of(a * per_plane, 8), per_plane)

    def up(t, a):
        return remote(part_sum.at[t, rows_of(a), :], from_low.at[t, rows_of(a), :],
                      lo_s.at[t, a], lo_r.at[t, a], row=(r + G) % n)

    def down(t, a):
        return remote(part_sum.at[t, rows_of(a), :], from_high.at[t, rows_of(a), :],
                      hi_s.at[t, a], hi_r.at[t, a], row=(r + n - G) % n)

    def f_send(t, k):
        mate = (q + k) % G
        return remote(fin.at[t, mate], out.at[:, x_cols(q, t)], f_s.at[t, k], f_r.at[t, q], row=z * G + mate)

    def f_from(t, k):
        mate = (q + k) % G
        return remote(fin.at[t, mate], out.at[:, x_cols(mate, t)], f_s.at[t, k], f_r.at[t, mate], row=z * G + mate)

    def f_own(t):
        return pltpu.make_async_copy(fin.at[t, q], out.at[:, x_cols(q, t)], f_s.at[t, 0])

    def multiply(t):
        x_own(t).wait()
        for k in (1, 3, 2):
            x_from(t, k).wait_recv()
        for s in range(G):
            for b in range(rows // BLOCK):
                span = slice(s * rows + b * BLOCK, s * rows + (b + 1) * BLOCK)
                for w in range(tw // BLOCK):
                    cols = slice(w * BLOCK, (w + 1) * BLOCK)
                    keep = jnp.broadcast_to(mrec[s, t, b:b + 1, w:w + 1], (BLOCK, BLOCK)).astype(BF16)
                    xmask[span, cols] = xrec[t, span, cols] * keep
        part_sum[t] = jnp.dot(hl[0], xmask[...], preferred_element_type=F32) + jnp.dot(
            hl[1], xmask[...], preferred_element_type=F32)

    def up_half(t, a):
        return remote(half_sum.at[t, rows_of(a), :], half_low.at[t, rows_of(a), :],
                      lo_s.at[t, a], lo_r.at[t, a], row=(r + G) % n)

    def down_half(t, a):
        return remote(half_sum.at[t, rows_of(a), :], half_high.at[t, rows_of(a), :],
                      hi_s.at[t, a], hi_r.at[t, a], row=(r + n - G) % n)

    def either(is_half, half, whole):
        if HALF:
            pl.when(is_half)(half)
            pl.when(jnp.logical_not(is_half))(whole)
        else:
            whole()

    def add(t, a, landed):
        part_sum[t, rows_of(a), :] += landed[t, rows_of(a), :].astype(F32)

    def take_up(t, a):
        def half():
            up_half(t, a).wait_recv()
            add(t, a, half_low)

        def whole():
            up(t, a).wait_recv()
            add(t, a, from_low)

        @pl.when(z > 0)
        def _():
            either(z == 1, half, whole)

    def take_down(t, a):
        def half():
            down_half(t, a).wait_recv()
            add(t, a, half_high)

        def whole():
            down(t, a).wait_recv()
            add(t, a, from_high)

        @pl.when(z < line - 1)
        def _():
            either(z == line - 2, half, whole)

    def forward(t):
        if HALF:
            @pl.when((z == 0) | (z == line - 1))
            def _():
                half_sum[t] = part_sum[t].astype(BF16)

        def go_up(i, carry):
            a = line - 1 - i
            take_up(t, a)
            either(z == 0, lambda: up_half(t, a).start(), lambda: up(t, a).start())
            return carry

        def go_down(a, carry):
            take_down(t, a)
            either(z == line - 1, lambda: down_half(t, a).start(), lambda: down(t, a).start())
            return carry

        @pl.when(z < line // 2)
        def _():
            lax.fori_loop(0, line - 1 - z, go_up, 0)

        lax.fori_loop(0, z, go_down, 0)

        @pl.when(z >= line // 2)
        def _():
            lax.fori_loop(0, line - 1 - z, go_up, 0)

    def finish(t):
        take_up(t, z)
        take_down(t, z)
        total = part_sum[t, rows_of(z), :] * factor
        for s in range(G):
            fin[t, s] = total[s * per_dev:(s + 1) * per_dev]
        f_own(t).start()
        for k in (2, 1, 3):
            f_send(t, k).start()

    def step(t, carry):
        multiply(t)
        forward(t)

        @pl.when(t > 0)
        def _():
            finish(t - 1)

        return carry

    lax.fori_loop(0, tiles, step, 0)
    finish(tiles - 1)

    @pl.loop(0, tiles)
    def _(t):
        f_own(t).wait()
        for k in range(1, G):
            f_from(t, k).wait_recv()
            f_send(t, k).wait_send()
            x_send(t, k).wait_send()

        def sent_up(a, carry):
            either(z == 0, lambda: up_half(t, a).wait_send(), lambda: up(t, a).wait_send())
            return carry

        def sent_down(a, carry):
            either(z == line - 1, lambda: down_half(t, a).wait_send(), lambda: down(t, a).wait_send())
            return carry

        lax.fori_loop(z + 1, line, sent_up, 0)
        lax.fori_loop(0, z, sent_down, 0)

    for k in range(1, G):
        m_send(k).wait_send()
        p_send(k).wait_send()

    @pl.loop(1, ncol)
    def _(j):
        c_own(j).wait_send()
        for k in range(1, G):
            c_relay(j, k).wait_send()

    @pl.loop(1, n)
    def _(k):
        to_owner(k).wait_send()
        to_source(k).wait_send()


def body(descriptors, block_mask, config_of):
    n, ncol = lax.axis_size("row"), lax.axis_size("col")
    rows, width = descriptors.shape
    row_blocks, blocks = block_mask.shape
    part = PW // ncol
    wide = -(-(part + 1) // 128) * 128
    chunk_blocks = blocks // G
    tiles = next(k for k in (TILES, 5, 1) if chunk_blocks % k == 0)
    per_tile = chunk_blocks // tiles
    tw = per_tile * BLOCK
    line = n // G
    per_dev = PW // n

    marks = block_mask.astype(F32).reshape(row_blocks, G, tiles, per_tile).transpose(1, 2, 0, 3)
    marks = jnp.pad(marks, ((0, 0), (0, 0), (0, 8 - row_blocks), (0, 128 - per_tile)))

    cfg = (n, ncol, rows, width, part, wide, tiles, tw, 1.0 / (rows * n))
    vm = pltpu.VMEM
    dma = pltpu.SemaphoreType.DMA
    half = vm((tiles, PW, tw) if HALF else (8, 128), BF16)
    full = pl.BlockSpec(memory_space=pltpu.VMEM)
    return pl.pallas_call(
        functools.partial(kernel, cfg),
        out_shape=jax.ShapeDtypeStruct((per_dev, width), F32),
        in_specs=[full, full, full, pl.BlockSpec(memory_space=pl.ANY)],
        out_specs=full,
        scratch_shapes=[
            vm((rows, wide), BF16),
            vm((n * SLOT, rows), BF16),
            vm((n * SLOT, wide), BF16),
            vm((n * SLOT, wide), BF16),
            vm((n * SLOT, 2 * wide), BF16),
            vm((n * SLOT, 2 * wide), BF16),
            vm((2, part, rows), BF16),
            vm((2, PW, G * rows), BF16),
            vm((G, tiles, 8, 128), F32),
            vm((tiles, G * rows, tw), BF16),
            vm((G * rows, tw), BF16),
            vm((tiles, PW, tw), F32),
            vm((tiles, PW, tw), F32),
            vm((tiles, PW, tw), F32),
            vm((tiles, G, per_dev, tw), F32),
            dma((n,)), dma((n,)), dma((n,)), dma((n,)),
            dma((G,)), dma((G,)), dma((ncol, G)), dma((ncol, G)),
            dma((G,)), dma((G,)), dma((tiles, G)), dma((tiles, G)),
            dma((tiles, line)), dma((tiles, line)), dma((tiles, line)), dma((tiles, line)),
            dma((tiles, G)), dma((tiles, G)), dma((5,)),
            half, half, half,
        ],
        compiler_params=pltpu.CompilerParams(
            collective_id=0, has_side_effects=True, vmem_limit_bytes=56 * 1024 * 1024),
    )(config_of[:, None], config_of[None, :], marks, descriptors)


def solution(mesh):
    in_specs = (P("row", "col"), P("row", "col"), P("row"))
    out_specs = P("row", "col")
    return jax.shard_map(body, mesh=mesh, in_specs=in_specs, out_specs=out_specs, check_vma=False)
```
